32 devices in a mesh: rows: 8 (over y, x, core), cols: 4 (over z).
Axes of the slice: x: 2, y: 2, z: 4, core: 2. Of those that a mesh axis runs over, the one named last changes fastest.
Arguments:
- matrix: float32 [16384, 512], P('rows', 'cols'), may hold values from -48 to 48
- partners: int32 [2, 4], replicated, may hold values from 0 to 3, each once within a row
Outputs:
- rotated: float32 [16384, 512], P('rows', 'cols')
The draws below stay inside these ranges and needn't reach their ends.
Inputs may be any that keep to these rules, and one draw needn't show every extreme that they name: Each row of partners names every block once.
All inputs are finite; a program needn't handle non-finite values.
Results may differ from the reference program's by a relative error of at most 0.00028.
Values sent between devices are 32-bit elements; how exact they have to be, the bound alone decides.
No kernel may reach another device: no remote copies, remote signals or barrier semaphores. Data moves between devices by JAX's collectives and lax.ppermute only.
A program may use at most 64 MiB of HBM per device.

```python
import jax
import jax.numpy as jnp
from jax import lax

BLOCK = 128
CYCLE = 3
MATCHED = 2
STEPS = 12
M = 16384
N = 512
N_COLS = 4


def draw_matrix(key, part):
    keys = jax.random.split(jax.random.fold_in(key, 71), 4)
    base = jnp.clip(jax.random.normal(keys[0], (M, N), jnp.float32), -5.0, 5.0)
    mixed = base + 0.5 * jnp.roll(base, -BLOCK, axis=1) + 0.4 * jnp.roll(base, -2 * BLOCK, axis=1) + 0.3 * jnp.roll(base, -3 * BLOCK, axis=1)
    common_rows = jnp.clip(jax.random.normal(keys[1], (M, 1), jnp.float32), -4.0, 4.0)
    common_cols = jnp.clip(jax.random.normal(keys[2], (1, N), jnp.float32), -4.0, 4.0)
    mixed = mixed + 0.3 * common_rows * common_cols
    colscale = jnp.exp(jax.random.uniform(keys[3], (1, N), jnp.float32, jnp.log(0.3), jnp.log(3.0)))
    return jnp.clip(mixed * colscale * 0.6, -48.0, 48.0)


def setup_inputs(seed: int = 0) -> dict:
    streams_of = jax.random.split(jax.random.key(seed), 3)
    matrix = draw_matrix(jax.random.fold_in(streams_of[2], 71), 0)
    partners = jax.vmap(lambda own: jax.random.permutation(own, N_COLS))(jax.random.split(streams_of[1], MATCHED)).reshape((MATCHED, N_COLS)).astype(jnp.int32)
    return dict(matrix=matrix, partners=partners)


epsilon = 1e-06
highest = lax.Precision.HIGHEST

def start_iterate(gram_full):
    order = gram_full.shape[0]
    scale = lax.rsqrt(jnp.diagonal(gram_full) + epsilon)
    normed = gram_full * scale[:, None] * scale[None, :]
    kernel = jnp.eye(order, dtype=jnp.float32) + jnp.triu(normed, 1) - jnp.tril(normed, -1)
    return kernel / jnp.sqrt(jnp.sum(kernel * kernel))

def polar_factor(start):

    def advance(counter, current):
        inner = jnp.dot(current.T, current, precision=highest)
        return 1.5 * current - 0.5 * jnp.dot(current, inner, precision=highest)
    return lax.fori_loop(0, STEPS, advance, start)

def reference(matrix, partners):
    blocks = matrix.reshape(M, N_COLS, BLOCK).transpose(1, 0, 2)
    for meeting in range(CYCLE + MATCHED):
        if meeting < CYCLE:
            order = (jnp.arange(N_COLS, dtype=jnp.int32) - (meeting + 1)) % N_COLS
        else:
            order = partners[meeting - CYCLE].astype(jnp.int32)

        def one_block(index, blocks=blocks, order=order):
            paired = jnp.concatenate([blocks[order[index]], blocks[index]], axis=1)
            gram_full = jnp.dot(paired.T, paired, precision=highest)
            rotation = polar_factor(start_iterate(gram_full))
            return jnp.dot(paired, rotation[:, BLOCK:], precision=highest)
        blocks = lax.map(one_block, jnp.arange(N_COLS, dtype=jnp.int32))
    return blocks.transpose(1, 0, 2).reshape(M, N)
```

```python
import functools

import jax
import jax.numpy as jnp
from jax import lax
from jax.experimental import pallas as pl
from jax.experimental.pallas import tpu as pltpu
from jax.sharding import PartitionSpec as P

CYCLE = 3
MATCHED = 2
STEPS = 12

epsilon = 1e-06
f32 = jnp.float32
bf16 = jnp.bfloat16

NN = (((1,), (0,)), ((), ()))
NT = (((1,), (1,)), ((), ()))
TN = (((0,), (0,)), ((), ()))


def split(x):
    high = x.astype(bf16)
    return high, (x - high.astype(f32)).astype(bf16)


def product(a, b, dims):
    def one(x, y):
        return lax.dot_general(x, y, dims, preferred_element_type=f32)

    return one(a[0], b[0]) + (one(a[0], b[1]) + one(a[1], b[0]))


def vmem():
    return pl.BlockSpec(memory_space=pltpu.VMEM)


def smem():
    return pl.BlockSpec(memory_space=pltpu.SMEM)


def stages_of(count):
    bits = count.bit_length() - 1
    if count != 1 << bits:
        return None
    groups, at = [], 0
    while at < bits:
        size = 1 if at == 0 else min(2, bits - at)
        groups.append((at, size))
        at += size
    return groups


def masks_of(stages):
    masks = [0]
    for at, size in stages:
        masks = [mask | (part << at) for mask in masks for part in range(1 << size)]
    return masks


def gram_kernel(groups, masks, piece, outs, place, own, *refs):
    others, out_refs = refs[: groups - 1], refs[groups - 1 : groups - 1 + outs]
    high, low, packed = refs[groups - 1 + outs :]
    row, col = place[0], place[1]
    width = own.shape[1]
    for distance, ref in enumerate((own, *others)):
        block = lax.rem(col - distance + groups, groups)
        high[block], low[block] = split(ref[...])
    at = 0
    for left in range(groups):
        for right in range(left, groups):
            packed[at : at + width, :] = product((high[left], low[left]), (high[right], low[right]), TN)
            at += width
    if at < packed.shape[0]:
        packed[at:, :] = jnp.zeros((packed.shape[0] - at, width), f32)
    each = len(masks) // outs
    for flat, mask in enumerate(masks):
        start = pl.multiple_of((row ^ mask) * piece, 8)
        out_refs[flat // each][flat % each] = packed[pl.ds(start, piece), :]


def partial_gram(place, matrix, others, groups, stages, piece):
    rows, width = matrix.shape
    quarter = rows // groups
    masks = masks_of(stages)
    outs = 1 << stages[0][1]
    shape = jax.ShapeDtypeStruct((len(masks) // outs, piece, width), f32)
    whole = pl.BlockSpec((quarter, width), lambda i, place: (0, 0))
    out_spec = pl.BlockSpec(shape.shape, lambda i, place: (0, 0, 0))
    return pl.pallas_call(
        functools.partial(gram_kernel, groups, masks, piece, outs),
        grid_spec=pltpu.PrefetchScalarGridSpec(
            num_scalar_prefetch=1,
            grid=(1,),
            in_specs=[pl.BlockSpec((quarter, width), lambda i, place: (place[1], 0))] + [whole] * (groups - 1),
            out_specs=[out_spec] * outs,
            scratch_shapes=[
                pltpu.VMEM((groups, quarter, width), bf16),
                pltpu.VMEM((groups, quarter, width), bf16),
                pltpu.VMEM((len(masks) * piece, width), f32),
            ],
        ),
        out_shape=[shape] * outs,
        name="gram",
    )(place, matrix, *others)


def meetings_kernel(groups, masks, piece, place, partners, *refs):
    pieces, out = refs[: len(masks)], refs[len(masks)]
    packed, gram, turn, mixed, made, high, low = refs[len(masks) + 1 :]
    row, col = place[0], place[1]
    width = out.shape[1]
    pair = 2 * width
    total = groups * width
    for mask, ref in zip(masks, pieces):
        packed[pl.ds(pl.multiple_of((row ^ mask) * piece, 8), piece), :] = ref[...]
    at = 0
    for left in range(groups):
        for right in range(left, groups):
            block = packed[at : at + width, :]
            gram[0, left, :, right * width : (right + 1) * width] = block
            if right > left:
                gram[0, right, :, left * width : (left + 1) * width] = block.T
            at += width
    row_at = lax.broadcasted_iota(jnp.int32, (width, width), 0)
    col_at = lax.broadcasted_iota(jnp.int32, (width, width), 1)
    same = jnp.where(row_at == col_at, 1.0, 0.0)
    for left in range(groups):
        for right in range(groups):
            turn[0, left, :, right * width : (right + 1) * width] = same if left == right else jnp.zeros_like(same)
    wide_row = lax.broadcasted_iota(jnp.int32, (pair, pair), 0)
    wide_col = lax.broadcasted_iota(jnp.int32, (pair, pair), 1)
    identity = jnp.where(wide_row == wide_col, 1.5, 0.0)

    def lanes(block):
        return pl.ds(pl.multiple_of(block * width, width), width)

    def partner(meeting, block):
        if isinstance(meeting, int) and meeting < CYCLE:
            return lax.rem(block - meeting - 1 + CYCLE * groups, groups)
        table = partners[jnp.maximum(meeting - CYCLE, 0), block]
        return jnp.where(meeting < CYCLE, lax.rem(block - meeting - 1 + CYCLE * groups, groups), table)

    def start(slot, now, other, block):
        oo, bb = gram[now, other, :, lanes(other)], gram[now, block, :, lanes(block)]
        ob, bo = gram[now, other, :, lanes(block)], gram[now, block, :, lanes(other)]

        def scales(x):
            diagonal = jnp.where(row_at == col_at, x, 0.0)
            across = jnp.sum(diagonal, axis=1, keepdims=True)
            down = jnp.sum(diagonal, axis=0, keepdims=True)
            return (lax.rsqrt(jnp.maximum(v, 0.0) + epsilon) for v in (across, down))

        (o_col, o_row), (b_col, b_row) = scales(oo), scales(bb)

        def normed(x, by_col, by_row):
            return jnp.clip(x * by_col * by_row, -1.0, 1.0)

        def skew(x, by_col, by_row):
            y = normed(x, by_col, by_row)
            return jnp.where(row_at == col_at, 1.0, jnp.where(row_at > col_at, y, -y))

        first = skew(oo, o_col, o_row), -normed(ob, o_col, b_row)
        second = normed(bo, b_col, o_row), skew(bb, b_col, b_row)
        squares = sum(jnp.sum(jnp.sum(x * x, axis=1, keepdims=True), axis=0, keepdims=True) for x in first + second)
        factor = 1.0 / jnp.sqrt(squares)
        for at, parts in ((0, first), (width, second)):
            for lane, part in ((0, parts[0]), (width, parts[1])):
                h, l = split(part * factor)
                high[slot, at : at + width, lane : lane + width] = h
                low[slot, at : at + width, lane : lane + width] = l

    def iterate(slots):
        def update(slot):
            x = high[slot], low[slot]
            return identity - 0.5 * product(x, x, NT)

        def advance(counter, carry):
            updates = [update(slot) for slot in range(slots)]
            for slot in range(slots):
                h, l = split(product(split(updates[slot]), (high[slot], low[slot]), NN))
                high[slot], low[slot] = h, l
            return carry

        lax.fori_loop(0, STEPS - 1, advance, 0)
        updates = [update(slot)[width:, :] for slot in range(slots)]
        return [split(product(split(updates[slot]), (high[slot], low[slot]), NN)) for slot in range(slots)]

    def stacked(ref, now, other, block):
        return jnp.concatenate([ref[now, other], ref[now, block]], axis=0)

    def meet(meeting, carry):
        now = lax.rem(meeting, 2)
        later = 1 - now
        order = [partner(meeting, block) for block in range(groups)]
        for block in range(groups):
            start(block, now, order[block], block)
        rotations = iterate(groups)
        for block in range(groups):
            mixed[block] = product(rotations[block], split(stacked(gram, now, order[block], block)), NN)
            turn[later, block] = product(rotations[block], split(stacked(turn, now, order[block], block)), NN)
        for block in range(groups):
            sides = jnp.concatenate(
                [
                    jnp.concatenate([mixed[left, :, lanes(order[block])], mixed[left, :, lanes(block)]], axis=1)
                    for left in range(groups)
                ],
                axis=0,
            )
            column = product(split(sides), rotations[block], NT)
            for left in range(groups):
                gram[later, left, :, block * width : (block + 1) * width] = column[left * width : (left + 1) * width]
        return carry

    last = CYCLE + MATCHED - 1
    lax.fori_loop(0, last, meet, 0)
    other = partner(last, col)
    start(0, last % 2, other, col)
    (rotation,) = iterate(1)
    made[...] = product(rotation, split(stacked(turn, last % 2, other, col)), NN)
    for distance in range(groups):
        out[distance] = made[:, lanes(lax.rem(col - distance + groups, groups))]


def meetings(place, partners, pieces, groups, stages, piece):
    width = pieces[0].shape[1]
    masks = masks_of(stages)
    total = groups * width
    return pl.pallas_call(
        functools.partial(meetings_kernel, groups, masks, piece),
        in_specs=[smem(), smem()] + [vmem()] * len(masks),
        out_specs=vmem(),
        out_shape=jax.ShapeDtypeStruct((groups, width, width), f32),
        scratch_shapes=[
            pltpu.VMEM((len(masks) * piece, width), f32),
            pltpu.VMEM((2, groups, width, total), f32),
            pltpu.VMEM((2, groups, width, total), f32),
            pltpu.VMEM((groups, width, total), f32),
            pltpu.VMEM((width, total), f32),
            pltpu.VMEM((groups, 2 * width, 2 * width), bf16),
            pltpu.VMEM((groups, 2 * width, 2 * width), bf16),
        ],
        name="meetings",
    )(place, partners, *pieces)


def apply_kernel(groups, place, turn, own, *refs):
    first, rest, out = refs[: groups - 1], refs[groups - 1 : 2 * groups - 2], refs[2 * groups - 2]
    step = pl.program_id(0)

    def apply(blocks):
        total = None
        for distance, block in enumerate(blocks):
            part = product(split(block[...]), split(turn[distance]), NT)
            total = part if total is None else total + part
        out[...] = total

    @pl.when(step == 0)
    def _():
        apply((own, *first))

    @pl.when(step > 0)
    def _():
        apply((own, *rest))


def apply_turn(place, turn, matrix, first, rest, groups):
    rows, width = matrix.shape
    quarter = rows // groups

    def own_map(i, place):
        return lax.rem(place[1] + i, groups), 0

    return pl.pallas_call(
        functools.partial(apply_kernel, groups),
        grid_spec=pltpu.PrefetchScalarGridSpec(
            num_scalar_prefetch=1,
            grid=(groups,),
            in_specs=[
                pl.BlockSpec((groups, width, width), lambda i, place: (0, 0, 0)),
                pl.BlockSpec((quarter, width), own_map),
            ]
            + [pl.BlockSpec((quarter, width), lambda i, place: (0, 0))] * (groups - 1)
            + [pl.BlockSpec((quarter, width), lambda i, place: (jnp.maximum(i - 1, 0), 0))] * (groups - 1),
            out_specs=pl.BlockSpec((quarter, width), own_map),
        ),
        out_shape=jax.ShapeDtypeStruct((rows, width), f32),
        name="apply",
    )(place, turn, matrix, *first, *rest)


def body(matrix, partners):
    rows, width = matrix.shape
    groups = lax.axis_size("cols")
    count = lax.axis_size("rows")
    stages = stages_of(count)
    quarter = rows // groups
    row, col = lax.axis_index("rows"), lax.axis_index("cols")
    place = jnp.stack([row, col]).astype(jnp.int32)

    def across(array, by):
        return lax.ppermute(array, "cols", [(i, (i + by) % groups) for i in range(groups)])

    def along(array, mask):
        return lax.ppermute(array, "rows", [(i, i ^ mask) for i in range(count)])

    first = [
        across(lax.dynamic_slice_in_dim(matrix, (col + by) % groups * quarter, quarter), by) for by in range(1, groups)
    ]
    packed_rows = groups * (groups + 1) // 2 * width
    piece = -(-packed_rows // (8 * count)) * 8
    parts = partial_gram(place, matrix, first, groups, stages, piece)
    held = None
    for level, (at, size) in enumerate(stages):
        if level:
            each = held.shape[0] >> size
            parts = [held[i * each : (i + 1) * each] for i in range(1 << size)]
        sent = [along(parts[part], part << at) for part in range(1, 1 << size)]
        held = parts[0]
        for array in sent:
            held = held + array
    held = held[0]
    far = [across(held, by) for by in range(1, groups)]
    for array in far:
        held = held + array
    held, matrix_later = lax.optimization_barrier((held, matrix))
    pieces = [held]
    for at, size in reversed(stages):
        pieces = [
            piece_ if part == 0 else along(piece_, part << at) for part in range(1 << size) for piece_ in pieces
        ]
    twice = jnp.concatenate([matrix_later, matrix_later])
    rest = [
        across(
            lax.dynamic_slice_in_dim(twice, ((col + by) % groups + 1) * quarter, rows - quarter),
            by,
        )
        for by in range(1, groups)
    ]
    turn = meetings(place, partners, pieces, groups, stages, piece)
    return apply_turn(place, turn, matrix, first, rest, groups)


def solution(mesh):
    placed = (P("rows", "cols"), P())
    return jax.shard_map(body, mesh=mesh, in_specs=placed, out_specs=P("rows", "cols"), check_vma=False)
```
